32 devices in a mesh: seq: 8 (over y, x, core), head: 4 (over z).
Axes of the slice: x: 2, y: 2, z: 4, core: 2. Of those that a mesh axis runs over, the one named last changes fastest.
Arguments:
- queries: bfloat16 [8192, 4096], P(('seq', 'head')), may hold values from -40 to 40
- keys: bfloat16 [8192, 4096], P(('seq', 'head')), may hold values from -4 to 4
- values: bfloat16 [8192, 4096], P(('seq', 'head')), may hold values from -40 to 40
- grad_out: bfloat16 [8192, 4096], P(('seq', 'head')), may hold values from -40 to 40
Outputs:
- output: bfloat16 [8192, 4096], P(('seq', 'head'))
- grad_queries: bfloat16 [8192, 4096], P(('seq', 'head'))
- grad_keys: bfloat16 [8192, 4096], P(('seq', 'head'))
- grad_values: bfloat16 [8192, 4096], P(('seq', 'head'))
The draws below stay inside these ranges and needn't reach their ends.
All inputs are finite; a program needn't handle non-finite values.
Results may differ from the reference program's by a relative error of at most 0.01.
Values may be sent and summed in bfloat16 or wider, within the bound.
No kernel may reach another device: no remote copies, remote signals or barrier semaphores. Data moves between devices by JAX's collectives and lax.ppermute only.
A program may use at most 128 MiB of HBM per device.

```python
import math
import jax
import jax.numpy as jnp
from jax import lax

HEADS = 32
DH = 128
L = 1024
D = 4096
TOKENS = 8192
N_SEQ = 8


def draw_queries(key, part):
    first, second = jax.random.split(jax.random.fold_in(key, 11))
    base = jnp.clip(jax.random.normal(first, (TOKENS, D), jnp.float32), -4.0, 4.0)
    scale = jnp.exp(jax.random.uniform(second, (TOKENS, 1), jnp.float32) * math.log(10.0))
    return (base * scale).astype(jnp.bfloat16)


def draw_values(key, part):
    first, second = jax.random.split(jax.random.fold_in(key, 23))
    base = jnp.clip(jax.random.normal(first, (TOKENS, D), jnp.float32), -4.0, 4.0)
    scale = jnp.exp(jax.random.uniform(second, (1, D), jnp.float32) * math.log(10.0))
    return (base * scale).astype(jnp.bfloat16)


def shard_levels(own_key, extent, cuts, least, top_value):
    loudness = 1.0
    for dim, shards_of in cuts:
        draws = jax.random.uniform(jax.random.fold_in(jax.random.fold_in(own_key, 6), dim), (shards_of,), jnp.float32, least / len(cuts), top_value / len(cuts))
        loudness = loudness * jnp.repeat(jnp.exp(draws), extent[dim] // shards_of).reshape((-1,) + (1,) * (len(extent) - 1 - dim))
    return loudness


def gaussian(own_key, dims, deviation, limit, shards=(), dtype=jnp.bfloat16):
    drawn = jax.random.normal(own_key, dims, jnp.float32) * deviation
    if len(shards) > 0:
        drawn = shard_levels(own_key, dims, shards, -0.22, 0.18) * drawn
    return jnp.clip(drawn, min=-limit, max=limit).astype(dtype)


def setup_inputs(seed: int = 0) -> dict:
    key_list = jax.random.split(jax.random.key(seed), 5)
    return {
        "queries": draw_queries(jax.random.fold_in(key_list[4], 71), 0),
        "keys": gaussian(key_list[1], (TOKENS, D), 1.0, 4.0, ((0, 32),)),
        "values": draw_values(jax.random.fold_in(key_list[4], 71), 0),
        "grad_out": gaussian(key_list[3], (TOKENS, D), 8.0, 40.0, ((0, 32),)),
    }


epsilon = 1e-06

def rounded(x):
    half = lax.optimization_barrier(x.astype(jnp.bfloat16))
    return half.astype(jnp.float32)

def feature_map(x):
    xf = x.astype(jnp.float32)
    return jnp.where(xf > 0, xf + 1.0, jnp.exp(jnp.minimum(xf, 0.0)))

def feature_slope(x):
    xf = x.astype(jnp.float32)
    return jnp.where(xf > 0, 1.0, jnp.exp(jnp.minimum(xf, 0.0)))

def block_core(query_blk, key_blk, value_blk, grad_blk, prefix_state):
    causal = jnp.arange(L)[:, None] >= jnp.arange(L)[None, :]
    query_feat = rounded(feature_map(query_blk))
    key_feat = rounded(feature_map(key_blk))
    value_f = value_blk.astype(jnp.float32)
    scores = jnp.einsum('thd,shd->hts', query_feat, key_feat)
    scores = rounded(jnp.where(causal[None], scores, 0.0))
    prefix_bf = rounded(prefix_state)
    mixed = jnp.einsum('hts,she->the', scores, value_f) + jnp.einsum('thd,hde->the', query_feat, prefix_bf)
    inv_rms = lax.rsqrt(lax.optimization_barrier(jnp.mean(mixed * mixed, -1, keepdims=True)) + epsilon)
    normed = mixed * inv_rms
    grad_norm = grad_blk.astype(jnp.float32)
    grad_mix = inv_rms * (grad_norm - normed * lax.optimization_barrier(jnp.mean(grad_norm * normed, -1, keepdims=True)))
    grad_mix = rounded(grad_mix)
    return (query_feat, key_feat, value_f, scores, prefix_bf, normed, grad_mix, causal)

def reference(queries, keys, values, grad_out):
    shape4 = (N_SEQ, L, HEADS, DH)
    query_blocks = queries.reshape(shape4)
    key_blocks = keys.reshape(shape4)
    value_blocks = values.reshape(shape4)
    grad_blocks = grad_out.reshape(shape4)

    def own_state(pair):
        key_feat = rounded(feature_map(pair[0]))
        return jnp.einsum('shd,she->hde', key_feat, pair[1].astype(jnp.float32))
    owns = lax.map(own_state, (key_blocks, value_blocks))
    running = jnp.cumsum(owns, 0)
    prefixes = jnp.concatenate([jnp.zeros_like(owns[:1]), running[:-1]], 0)

    def first_pass(items):
        core = block_core(*items)
        query_state = jnp.einsum('thd,the->hde', core[0], core[6])
        return (core[5].astype(jnp.bfloat16), query_state)
    normed_blocks, query_states = lax.map(first_pass, (query_blocks, key_blocks, value_blocks, grad_blocks, prefixes))
    backward_sum = jnp.cumsum(query_states[::-1], 0)[::-1]
    suffixes = jnp.concatenate([backward_sum[1:], jnp.zeros_like(query_states[:1])], 0)

    def second_pass(items):
        query_feat, key_feat, value_f, scores, prefix_bf, normed, grad_mix, causal = block_core(*items[:5])
        suffix_bf = rounded(items[5])
        grad_scores = jnp.einsum('the,she->hts', grad_mix, value_f)
        grad_scores = rounded(jnp.where(causal[None], grad_scores, 0.0))
        grad_qf = jnp.einsum('the,hde->thd', grad_mix, prefix_bf) + jnp.einsum('hts,shd->thd', grad_scores, key_feat)
        grad_kf = jnp.einsum('she,hde->shd', value_f, suffix_bf) + jnp.einsum('hts,thd->shd', grad_scores, query_feat)
        grad_vf = jnp.einsum('shd,hde->she', key_feat, suffix_bf) + jnp.einsum('hts,the->she', scores, grad_mix)
        grad_q = (grad_qf * feature_slope(items[0])).astype(jnp.bfloat16)
        grad_k = (grad_kf * feature_slope(items[1])).astype(jnp.bfloat16)
        return (grad_q, grad_k, grad_vf.astype(jnp.bfloat16))
    grad_q, grad_k, grad_v = lax.map(second_pass, (query_blocks, key_blocks, value_blocks, grad_blocks, prefixes, suffixes))
    flat = (TOKENS, D)
    return (normed_blocks.reshape(flat), grad_q.reshape(flat), grad_k.reshape(flat), grad_v.reshape(flat))
```

```python
import functools

import jax
import jax.numpy as jnp
from jax import lax
from jax.experimental import pallas as pl
from jax.experimental.pallas import tpu as pltpu
from jax.sharding import PartitionSpec as P

DH = 128
EPSILON = 1e-06
AXES = ("seq", "head")
F32 = jnp.float32
BF16 = jnp.bfloat16


def feature(x):
    xf = x.astype(F32)
    return jnp.where(xf > 0, xf + 1.0, jnp.exp(jnp.minimum(xf, 0.0)))


def slope(x):
    xf = x.astype(F32)
    return jnp.where(xf > 0, 1.0, jnp.exp(jnp.minimum(xf, 0.0)))


def dot(a, b, ca, cb):
    return lax.dot_general(a, b, (((ca,), (cb,)), ((), ())), preferred_element_type=F32)


def causal_mask(rows):
    t = lax.broadcasted_iota(jnp.int32, (rows, rows), 0)
    s = lax.broadcasted_iota(jnp.int32, (rows, rows), 1)
    return t >= s


def cols(j):
    return pl.ds(j * DH, DH)


def own_kernel(hb, k_ref, v_ref, s_ref):
    for j in range(hb):
        k = feature(k_ref[:, cols(j)]).astype(BF16)
        s_ref[cols(j), :] = dot(k, v_ref[:, cols(j)], 0, 0).astype(BF16)


def pre_kernel(hb, q_ref, k_ref, v_ref, ml_ref):
    mask = causal_mask(q_ref.shape[0])
    for j in range(hb):
        q = feature(q_ref[:, cols(j)]).astype(BF16)
        k = feature(k_ref[:, cols(j)]).astype(BF16)
        a = jnp.where(mask, dot(q, k, 1, 1), 0.0).astype(BF16)
        ml_ref[:, cols(j)] = dot(a, v_ref[:, cols(j)], 1, 0)


def fwd_kernel(hb, q_ref, g_ref, ml_ref, p_ref, out_ref, gy_ref, qg_ref):
    for j in range(hb):
        q = feature(q_ref[:, cols(j)]).astype(BF16)
        mixed = ml_ref[:, cols(j)] + dot(q, p_ref[cols(j), :], 1, 0)
        inv = lax.rsqrt(jnp.mean(mixed * mixed, -1, keepdims=True) + EPSILON)
        normed = mixed * inv
        g = g_ref[:, cols(j)].astype(F32)
        gy = inv * (g - normed * jnp.mean(g * normed, -1, keepdims=True))
        gy = gy.astype(BF16)
        out_ref[:, cols(j)] = normed.astype(BF16)
        gy_ref[:, cols(j)] = gy
        qg_ref[cols(j), :] = dot(q, gy, 0, 0).astype(BF16)


def mid_kernel(hb, q_ref, k_ref, v_ref, gy_ref, p_ref, dq_ref, dk_ref, dv_ref):
    mask = causal_mask(q_ref.shape[0])
    for j in range(hb):
        q_raw = q_ref[:, cols(j)]
        q = feature(q_raw).astype(BF16)
        k = feature(k_ref[:, cols(j)]).astype(BF16)
        gy = gy_ref[:, cols(j)]
        m = jnp.where(mask, dot(gy, v_ref[:, cols(j)], 1, 1), 0.0).astype(BF16)
        a = jnp.where(mask, dot(q, k, 1, 1), 0.0).astype(BF16)
        dq = dot(gy, p_ref[cols(j), :], 1, 1) + dot(m, k, 1, 0)
        dq_ref[:, cols(j)] = (dq * slope(q_raw)).astype(BF16)
        dk_ref[:, cols(j)] = dot(m, q, 0, 0)
        dv_ref[:, cols(j)] = dot(a, gy, 0, 0)


def last_kernel(hb, k_ref, v_ref, u_ref, dk_ref, dv_ref, gk_ref, gv_ref):
    for j in range(hb):
        k_raw = k_ref[:, cols(j)]
        k = feature(k_raw).astype(BF16)
        u = u_ref[cols(j), :]
        dk = dk_ref[:, cols(j)] + dot(v_ref[:, cols(j)], u, 1, 1)
        gk_ref[:, cols(j)] = (dk * slope(k_raw)).astype(BF16)
        gv_ref[:, cols(j)] = (dv_ref[:, cols(j)] + dot(k, u, 1, 0)).astype(BF16)


def scan_kernel(n, reverse, x_ref, o_ref):
    r = x_ref.shape[0] // n
    total = jnp.zeros((r, DH), F32)
    for i in range(n):
        at = pl.ds((n - 1 - i if reverse else i) * r, r)
        o_ref[at, :] = total.astype(BF16)
        total = total + x_ref[at, :].astype(F32)


def exclusive_scan(state, n, reverse):
    rows = state.shape[0]
    x = lax.all_to_all(state, AXES, 0, 0, tiled=True)
    vm = pl.BlockSpec(memory_space=pltpu.VMEM)
    y = pl.pallas_call(
        functools.partial(scan_kernel, n, reverse),
        out_shape=jax.ShapeDtypeStruct((rows, DH), BF16),
        in_specs=[vm],
        out_specs=vm,
        name="scan",
    )(x)
    return lax.all_to_all(y, AXES, 0, 0, tiled=True)


def local(queries, keys, values, grad_out):
    n = lax.axis_size("seq") * lax.axis_size("head")
    rows, width = queries.shape
    heads = width // DH
    hb = 4
    tok = pl.BlockSpec((rows, hb * DH), lambda i: (0, i))
    st = pl.BlockSpec((hb * DH, DH), lambda i: (i, 0))
    wide = lambda dt: jax.ShapeDtypeStruct((rows, width), dt)
    state = jax.ShapeDtypeStruct((width, DH), BF16)

    def call(kernel, ins, outs, shapes, name, flops, nbytes):
        return pl.pallas_call(
            functools.partial(kernel, hb),
            grid=(heads // hb,),
            in_specs=ins,
            out_specs=outs,
            out_shape=shapes,
            name=name,
            cost_estimate=pl.CostEstimate(
                flops=flops * heads * rows * DH, bytes_accessed=nbytes * rows * width, transcendentals=0
            ),
        )

    own = call(own_kernel, [tok, tok], st, state, "own", 2 * DH, 5)(keys, values)
    prefix = exclusive_scan(own, n, False)
    mixed_local = call(pre_kernel, [tok] * 3, tok, wide(F32), "pre", 4 * rows, 10)(queries, keys, values)
    output, gy, qg = call(
        fwd_kernel, [tok, tok, tok, st], [tok, tok, st], [wide(BF16), wide(BF16), state], "fwd", 4 * DH, 14
    )(queries, grad_out, mixed_local, prefix)
    suffix = exclusive_scan(qg, n, True)
    grad_q, dk, dv = call(
        mid_kernel, [tok] * 4 + [st], [tok] * 3, [wide(BF16), wide(F32), wide(F32)], "mid", 10 * rows + 2 * DH, 20
    )(queries, keys, values, gy, prefix)
    grad_k, grad_v = call(
        last_kernel, [tok, tok, st, tok, tok], [tok, tok], [wide(BF16), wide(BF16)], "last", 4 * DH, 17
    )(keys, values, suffix, dk, dv)
    return (output, grad_q, grad_k, grad_v)


def solution(mesh):
    placed = (P(AXES, None),) * 4
    return jax.shard_map(local, mesh=mesh, in_specs=placed, out_specs=placed, check_vma=False)
```

```python
import functools

import jax
import jax.numpy as jnp
from jax import lax
from jax.experimental import pallas as pl
from jax.experimental.pallas import tpu as pltpu
from jax.sharding import PartitionSpec as P

DH = 128
EPSILON = 1e-06
AXES = ("seq", "head")
F32 = jnp.float32
BF16 = jnp.bfloat16
STEP = 8
VMEM_LIMIT = 24 * 1024 * 1024


def feature(x):
    return jnp.where(x > 0, x + jnp.ones((), BF16), jnp.exp(x.astype(F32)).astype(BF16))


def feature_slope(x):
    xf = x.astype(F32)
    up = xf > 0
    e = jnp.exp(jnp.minimum(xf, 0.0))
    return jnp.where(up, xf + 1.0, e).astype(BF16), jnp.where(up, 1.0, e)


def dot(a, b, ca, cb):
    return lax.dot_general(a, b, (((ca,), (cb,)), ((), ())), preferred_element_type=F32)


def causal_mask(rows):
    t = lax.broadcasted_iota(jnp.int32, (rows, rows), 0)
    s = lax.broadcasted_iota(jnp.int32, (rows, rows), 1)
    return t >= s


def own_body(k, v):
    return (dot(feature(k), v, 0, 0).astype(BF16),)


def pre_body(q, k, v):
    qf = feature(q)
    kf = feature(k)
    a = jnp.where(causal_mask(q.shape[0]), dot(qf, kf, 1, 1), 0.0).astype(BF16)
    return (dot(a, v, 1, 0).astype(BF16),)


def fwd_body(q, g, mixed_local, p):
    qf = feature(q)
    mixed = mixed_local.astype(F32) + dot(qf, p, 1, 0)
    gf = g.astype(F32)
    inv = lax.rsqrt(jnp.mean(mixed * mixed, -1, keepdims=True) + EPSILON)
    normed = mixed * inv
    gy = (inv * (gf - normed * jnp.mean(gf * normed, -1, keepdims=True))).astype(BF16)
    return normed.astype(BF16), gy, dot(qf, gy, 0, 0).astype(BF16)


def mid_body(q, k, v, gy, p):
    qf, q_slope = feature_slope(q)
    kf = feature(k)
    mask = causal_mask(q.shape[0])
    m = jnp.where(mask, dot(gy, v, 1, 1), 0.0).astype(BF16)
    a = jnp.where(mask, dot(qf, kf, 1, 1), 0.0).astype(BF16)
    dq = dot(gy, p, 1, 1) + dot(m, kf, 1, 0)
    return (dq * q_slope).astype(BF16), dot(m, qf, 0, 0).astype(BF16), dot(a, gy, 0, 0).astype(BF16)


def last_body(k, v, u, dk, dv):
    kf, k_slope = feature_slope(k)
    dk = dk.astype(F32) + dot(v, u, 1, 1)
    dv = dv.astype(F32) + dot(kf, u, 1, 0)
    return (dk * k_slope).astype(BF16), dv.astype(BF16)


def chunk(ref, at, size, tall):
    piece = pl.ds(pl.multiple_of(at * size, size), size)
    return ref.at[piece, :] if tall else ref.at[:, piece]


def stream_kernel(body, step, tall_in, tall_out, held_in, held_out, *refs):
    refs = list(refs)
    take = lambda count: [refs.pop(0) for _ in range(count)]
    ni, no = len(tall_in), len(tall_out)
    ins, outs = take(ni), take(no)
    in_bufs = [r if held else refs.pop(0) for r, held in zip(ins, held_in)]
    out_bufs = [r if held else refs.pop(0) for r, held in zip(outs, held_out)]
    in_sem, out_sem = refs
    moved_in = [i for i in range(ni) if not held_in[i]]
    moved_out = [i for i in range(no) if not held_out[i]]
    size = step * DH
    steps = in_bufs[0].shape[0 if tall_in[0] else 1] // size

    def fetch(i, c):
        return pltpu.make_async_copy(
            chunk(ins[i], c, size, tall_in[i]), chunk(in_bufs[i], c, size, tall_in[i]), in_sem.at[i, c]
        )

    def put(i, c):
        return pltpu.make_async_copy(
            chunk(out_bufs[i], c, size, tall_out[i]), chunk(outs[i], c, size, tall_out[i]), out_sem.at[i, c]
        )

    @pl.loop(0, steps)
    def _(c):
        for i in moved_in:
            fetch(i, c).start()

    @pl.loop(0, steps)
    def _(c):
        for i in moved_in:
            fetch(i, c).wait()
        for j in range(step):
            at = c * step + j
            values = [chunk(in_bufs[i], at, DH, tall_in[i])[...] for i in range(ni)]
            for i, value in enumerate(body(*values)):
                chunk(out_bufs[i], at, DH, tall_out[i])[...] = value
        for i in moved_out:
            put(i, c).start()

    @pl.loop(0, steps)
    def _(c):
        for i in moved_out:
            put(i, c).wait()


def stream(body, name, args, outs, step, flops, held_in=(), held_out=()):
    width = args[0].shape[1]
    held_in = [i in held_in for i in range(len(args))]
    held_out = [i in held_out for i in range(len(outs))]
    tall_in = [a.shape[1] == DH for a in args]
    tall_out = [o.shape[1] == DH for o in outs]
    steps = width // DH // step
    nbytes = sum(a.size * a.dtype.itemsize for a in args) + sum(o.size * o.dtype.itemsize for o in outs)
    spec = lambda held: pl.BlockSpec(memory_space=pltpu.VMEM if held else pltpu.HBM)
    place = lambda a, held: pltpu.with_memory_space_constraint(a, pltpu.VMEM if held else pltpu.HBM)
    bufs = [pltpu.VMEM(a.shape, a.dtype) for a, h in zip(args, held_in) if not h]
    bufs += [pltpu.VMEM(o.shape, o.dtype) for o, h in zip(outs, held_out) if not h]
    return pl.pallas_call(
        functools.partial(stream_kernel, body, step, tall_in, tall_out, held_in, held_out),
        in_specs=[spec(h) for h in held_in],
        out_specs=[spec(h) for h in held_out],
        out_shape=[(pltpu.VMEM if h else pltpu.HBM)(o.shape, o.dtype) for o, h in zip(outs, held_out)],
        scratch_shapes=bufs
        + [pltpu.SemaphoreType.DMA((len(args), steps)), pltpu.SemaphoreType.DMA((len(outs), steps))],
        name=name,
        compiler_params=pltpu.CompilerParams(vmem_limit_bytes=VMEM_LIMIT),
        cost_estimate=pl.CostEstimate(
            flops=flops * width * args[0].shape[0], bytes_accessed=nbytes, transcendentals=0
        ),
    )(*[place(a, h) for a, h in zip(args, held_in)])


def scan_kernel(n, reverse, x_ref, o_ref, buf, sem):
    r = x_ref.shape[0] // n
    parts = 4 if n % 4 == 0 else 1
    span = n // parts
    total = jnp.zeros((r, DH), F32)
    copies = []
    for part in range(parts):
        for i in range(part * span, (part + 1) * span):
            at = pl.ds((n - 1 - i if reverse else i) * r, r)
            buf[at, :] = total.astype(BF16)
            total = total + x_ref[at, :].astype(F32)
        at = pl.ds((parts - 1 - part if reverse else part) * span * r, span * r)
        copies.append(pltpu.make_async_copy(buf.at[at, :], o_ref.at[at, :], sem.at[part]))
        copies[-1].start()
    for copy in copies:
        copy.wait()


def exclusive_scan(state, n, reverse):
    rows = state.shape[0]
    x = lax.all_to_all(state, AXES, 0, 0, tiled=True)
    y = pl.pallas_call(
        functools.partial(scan_kernel, n, reverse),
        out_shape=pltpu.HBM((rows, DH), BF16),
        in_specs=[pl.BlockSpec(memory_space=pltpu.VMEM)],
        out_specs=pl.BlockSpec(memory_space=pltpu.HBM),
        scratch_shapes=[pltpu.VMEM((rows, DH), BF16), pltpu.SemaphoreType.DMA((4,))],
        name="scan",
        compiler_params=pltpu.CompilerParams(vmem_limit_bytes=VMEM_LIMIT),
    )(pltpu.with_memory_space_constraint(x, pltpu.VMEM))
    return lax.all_to_all(y, AXES, 0, 0, tiled=True)


def local(queries, keys, values, grad_out):
    n = lax.axis_size("seq") * lax.axis_size("head")
    rows, width = queries.shape
    wide = lambda dt: jax.ShapeDtypeStruct((rows, width), dt)
    state = jax.ShapeDtypeStruct((width, DH), BF16)

    (own,) = stream(own_body, "own", [keys, values], [state], STEP, 2 * DH)
    prefix = exclusive_scan(own, n, False)
    (mixed_local,) = stream(pre_body, "pre", [queries, keys, values], [wide(BF16)], STEP, 4 * rows)
    output, gy, qg = stream(
        fwd_body,
        "fwd",
        [queries, grad_out, mixed_local, prefix],
        [wide(BF16), wide(BF16), state],
        STEP,
        4 * DH,
        (3,),
    )
    suffix = exclusive_scan(qg, n, True)
    grad_q, dk, dv = stream(
        mid_body, "mid", [queries, keys, values, gy, prefix], [wide(BF16), wide(BF16), wide(BF16)], STEP, 10 * rows
    )
    grad_k, grad_v = stream(
        last_body, "last", [keys, values, suffix, dk, dv], [wide(BF16), wide(BF16)], STEP, 4 * DH, (2,)
    )
    return (output, grad_q, grad_k, grad_v)


def solution(mesh):
    placed = (P(AXES, None),) * 4
    return jax.shard_map(local, mesh=mesh, in_specs=placed, out_specs=placed, check_vma=False)
```

```python
import functools

import jax
import jax.numpy as jnp
from jax import lax
from jax.experimental import pallas as pl
from jax.experimental.pallas import tpu as pltpu
from jax.sharding import PartitionSpec as P

DH = 128
EPSILON = 1e-06
AXES = ("seq", "head")
F32 = jnp.float32
BF16 = jnp.bfloat16
STEP = 8
VMEM_LIMIT = 24 * 1024 * 1024


def feature(x):
    return jnp.where(x > 0, x + jnp.ones((), BF16), jnp.exp(x.astype(F32)).astype(BF16))


def feature_slope(x):
    xf = x.astype(F32)
    up = xf > 0
    e = jnp.exp(jnp.minimum(xf, 0.0))
    return jnp.where(up, xf + 1.0, e).astype(BF16), jnp.where(up, 1.0, e)


def dot(a, b, ca, cb):
    return lax.dot_general(a, b, (((ca,), (cb,)), ((), ())), preferred_element_type=F32)


def causal_mask(rows):
    t = lax.broadcasted_iota(jnp.int32, (rows, rows), 0)
    s = lax.broadcasted_iota(jnp.int32, (rows, rows), 1)
    return t >= s


def own_body(k, v):
    return (dot(v, feature(k), 0, 0).astype(BF16),)


def pre_body(q, k, v, g):
    qf = feature(q)
    a = jnp.where(causal_mask(q.shape[0]), dot(qf, feature(k), 1, 1), 0.0).astype(BF16)
    return dot(v, a, 0, 1).astype(BF16), g.T, qf


def normalize(qf, g, mixed_local, p):
    cuts = [slice(i, i + DH) for i in range(0, p.shape[0], DH)]
    shape = (len(cuts), DH, qf.shape[0])
    mixed = mixed_local.astype(F32) + jnp.concatenate([dot(p[h], qf[:, h], 1, 1) for h in cuts], 0)
    mixed = mixed.reshape(shape)
    gf = g.astype(F32).reshape(shape)
    inv = lax.rsqrt(jnp.mean(mixed * mixed, 1, keepdims=True) + EPSILON)
    gy = inv * (gf - mixed * (inv * (inv * jnp.mean(gf * mixed, 1, keepdims=True))))
    return mixed * inv, gy.astype(BF16)


def fwd_body(qf, g, mixed_local, p):
    _, gy = normalize(qf, g, mixed_local, p)
    states = [dot(gy[i], qf[:, i * DH : (i + 1) * DH], 1, 0) for i in range(gy.shape[0])]
    return (jnp.concatenate(states, 0).astype(BF16),)


def mid_body(q, k, v, g, mixed_local, p):
    qf, q_slope = feature_slope(q)
    normed, gy = normalize(qf, g, mixed_local, p)
    kf = feature(k)
    gy = gy[0].T
    mask = causal_mask(q.shape[0])
    m = jnp.where(mask, dot(gy, v, 1, 1), 0.0).astype(BF16)
    a = jnp.where(mask, dot(qf, kf, 1, 1), 0.0).astype(BF16)
    dq = dot(gy, p, 1, 0) + dot(m, kf, 1, 0)
    output = normed[0].astype(BF16).T
    return output, (dq * q_slope).astype(BF16), dot(m, qf, 0, 0).astype(BF16), dot(a, gy, 0, 0).astype(BF16)


def last_body(k, v, u, dk, dv):
    kf, k_slope = feature_slope(k)
    dk = dk.astype(F32) + dot(v, u, 1, 0)
    dv = dv.astype(F32) + dot(kf, u, 1, 1)
    return (dk * k_slope).astype(BF16), dv.astype(BF16)


def chunk(ref, at, size, tall):
    piece = pl.ds(pl.multiple_of(at * size, size), size)
    return ref.at[piece, :] if tall else ref.at[:, piece]


def stream_kernel(body, step, together, tall_in, tall_out, held_in, held_out, *refs):
    refs = list(refs)
    take = lambda count: [refs.pop(0) for _ in range(count)]
    ni, no = len(tall_in), len(tall_out)
    ins, outs = take(ni), take(no)
    in_bufs = [r if held else refs.pop(0) for r, held in zip(ins, held_in)]
    out_bufs = [r if held else refs.pop(0) for r, held in zip(outs, held_out)]
    in_sem, out_sem = refs
    moved_in = [i for i in range(ni) if not held_in[i]]
    moved_out = [i for i in range(no) if not held_out[i]]
    size = step * DH
    steps = in_bufs[0].shape[0 if tall_in[0] else 1] // size

    def fetch(i, c):
        return pltpu.make_async_copy(
            chunk(ins[i], c, size, tall_in[i]), chunk(in_bufs[i], c, size, tall_in[i]), in_sem.at[i, c]
        )

    def put(i, c):
        return pltpu.make_async_copy(
            chunk(out_bufs[i], c, size, tall_out[i]), chunk(outs[i], c, size, tall_out[i]), out_sem.at[i, c]
        )

    @pl.loop(0, steps)
    def _(c):
        for i in moved_in:
            fetch(i, c).start()

    @pl.loop(0, steps)
    def _(c):
        for i in moved_in:
            fetch(i, c).wait()
        span = together * DH
        for j in range(step // together):
            at = c * (step // together) + j
            values = [chunk(in_bufs[i], at, span, tall_in[i])[...] for i in range(ni)]
            for i, value in enumerate(body(*values)):
                chunk(out_bufs[i], at, span, tall_out[i])[...] = value
        for i in moved_out:
            put(i, c).start()

    @pl.loop(0, steps)
    def _(c):
        for i in moved_out:
            put(i, c).wait()


def stream(body, name, args, outs, step, flops, held_in=(), held_out=(), together=1):
    width = args[0].shape[1]
    held_in = [i in held_in for i in range(len(args))]
    held_out = [i in held_out for i in range(len(outs))]
    tall_in = [a.shape[0] == width for a in args]
    tall_out = [o.shape[0] == width for o in outs]
    steps = width // DH // step
    nbytes = sum(a.size * a.dtype.itemsize for a in args) + sum(o.size * o.dtype.itemsize for o in outs)
    spec = lambda held: pl.BlockSpec(memory_space=pltpu.VMEM if held else pltpu.HBM)
    place = lambda a, held: pltpu.with_memory_space_constraint(a, pltpu.VMEM if held else pltpu.HBM)
    bufs = [pltpu.VMEM(a.shape, a.dtype) for a, h in zip(args, held_in) if not h]
    bufs += [pltpu.VMEM(o.shape, o.dtype) for o, h in zip(outs, held_out) if not h]
    return pl.pallas_call(
        functools.partial(stream_kernel, body, step, together, tall_in, tall_out, held_in, held_out),
        in_specs=[spec(h) for h in held_in],
        out_specs=[spec(h) for h in held_out],
        out_shape=[(pltpu.VMEM if h else pltpu.HBM)(o.shape, o.dtype) for o, h in zip(outs, held_out)],
        scratch_shapes=bufs
        + [pltpu.SemaphoreType.DMA((len(args), steps)), pltpu.SemaphoreType.DMA((len(outs), steps))],
        name=name,
        compiler_params=pltpu.CompilerParams(vmem_limit_bytes=VMEM_LIMIT),
        cost_estimate=pl.CostEstimate(
            flops=flops * width * args[0].shape[0], bytes_accessed=nbytes, transcendentals=0
        ),
    )(*[place(a, h) for a, h in zip(args, held_in)])


def scan_kernel(n, reverse, x_ref, o_ref, buf, sem):
    r = x_ref.shape[0] // n
    parts = 4 if n % 4 == 0 else 1
    span = n // parts
    total = jnp.zeros((r, DH), F32)
    copies = []
    for part in range(parts):
        for i in range(part * span, (part + 1) * span):
            at = pl.ds((n - 1 - i if reverse else i) * r, r)
            buf[at, :] = total.astype(BF16)
            total = total + x_ref[at, :].astype(F32)
        at = pl.ds((parts - 1 - part if reverse else part) * span * r, span * r)
        copies.append(pltpu.make_async_copy(buf.at[at, :], o_ref.at[at, :], sem.at[part]))
        copies[-1].start()
    for copy in copies:
        copy.wait()


def exclusive_scan(state, n, reverse):
    rows = state.shape[0]
    x = lax.all_to_all(state, AXES, 0, 0, tiled=True)
    y = pl.pallas_call(
        functools.partial(scan_kernel, n, reverse),
        out_shape=pltpu.HBM((rows, DH), BF16),
        in_specs=[pl.BlockSpec(memory_space=pltpu.VMEM)],
        out_specs=pl.BlockSpec(memory_space=pltpu.HBM),
        scratch_shapes=[pltpu.VMEM((rows, DH), BF16), pltpu.SemaphoreType.DMA((4,))],
        name="scan",
        compiler_params=pltpu.CompilerParams(vmem_limit_bytes=VMEM_LIMIT),
    )(pltpu.with_memory_space_constraint(x, pltpu.VMEM))
    return lax.all_to_all(y, AXES, 0, 0, tiled=True)


def local(queries, keys, values, grad_out):
    n = lax.axis_size("seq") * lax.axis_size("head")
    rows, width = queries.shape
    wide = lambda dt: jax.ShapeDtypeStruct((rows, width), dt)
    state = jax.ShapeDtypeStruct((width, DH), BF16)

    turned = jax.ShapeDtypeStruct((width, rows), BF16)
    (own,) = stream(own_body, "own", [keys, values], [state], STEP, 2 * DH)
    prefix = exclusive_scan(own, n, False)
    mixed_local, grad_turned, query_feat = stream(
        pre_body, "pre", [queries, keys, values, grad_out], [turned, turned, wide(BF16)], STEP, 4 * rows
    )
    (qg,) = stream(fwd_body, "fwd", [query_feat, grad_turned, mixed_local, prefix], [state], STEP, 4 * DH, (3,), together=STEP)
    suffix = exclusive_scan(qg, n, True)
    output, grad_q, dk, dv = stream(
        mid_body, "mid", [queries, keys, values, grad_turned, mixed_local, prefix], [wide(BF16)] * 4, STEP, 10 * rows
    )
    grad_k, grad_v = stream(
        last_body, "last", [keys, values, suffix, dk, dv], [wide(BF16), wide(BF16)], STEP, 4 * DH, (2,)
    )
    return (output, grad_q, grad_k, grad_v)


def solution(mesh):
    placed = (P(AXES, None),) * 4
    return jax.shard_map(local, mesh=mesh, in_specs=placed, out_specs=placed, check_vma=False)
```

```python
import functools

import jax
import jax.numpy as jnp
from jax import lax
from jax.experimental import pallas as pl
from jax.experimental.pallas import tpu as pltpu
from jax.sharding import PartitionSpec as P

DH = 128
EPSILON = 1e-06
AXES = ("seq", "head")
F32 = jnp.float32
BF16 = jnp.bfloat16
STEP = 8
VMEM_LIMIT = 24 * 1024 * 1024


def feature(x):
    return jnp.where(x > 0, x + jnp.ones((), BF16), jnp.exp(x.astype(F32)).astype(BF16))


def feature_slope(x):
    xf = x.astype(F32)
    up = xf > 0
    e = jnp.exp(jnp.minimum(xf, 0.0))
    return jnp.where(up, xf + 1.0, e).astype(BF16), jnp.where(up, 1.0, e)


def dot(a, b, ca, cb):
    return lax.dot_general(a, b, (((ca,), (cb,)), ((), ())), preferred_element_type=F32)


def causal_mask(rows):
    t = lax.broadcasted_iota(jnp.int32, (rows, rows), 0)
    s = lax.broadcasted_iota(jnp.int32, (rows, rows), 1)
    return t >= s


def own_body(k, v):
    cuts = [slice(i, i + DH) for i in range(0, k.shape[1], DH)]
    kf = feature(k)
    return (jnp.concatenate([dot(v[:, h], kf[:, h], 0, 0) for h in cuts], 0).astype(BF16),)


def pre_body(q, k, v, g):
    qf = feature(q)
    kf = feature(k)
    a = jnp.where(causal_mask(q.shape[0]), dot(qf, kf, 1, 1), 0.0).astype(BF16)
    return dot(v, a, 0, 1).astype(BF16), g.T, qf, kf


def normalize(qf, g, mixed_local, p):
    cuts = [slice(i, i + DH) for i in range(0, p.shape[0], DH)]
    shape = (len(cuts), DH, qf.shape[0])
    mixed = mixed_local.astype(F32) + jnp.concatenate([dot(p[h], qf[:, h], 1, 1) for h in cuts], 0)
    mixed = mixed.reshape(shape)
    gf = g.astype(F32).reshape(shape)
    inv = lax.rsqrt(jnp.mean(mixed * mixed, 1, keepdims=True) + EPSILON)
    gy = inv * (gf - mixed * (inv * (inv * jnp.mean(gf * mixed, 1, keepdims=True))))
    return mixed * inv, gy.astype(BF16)


def fwd_body(qf, g, mixed_local, p):
    _, gy = normalize(qf, g, mixed_local, p)
    states = [dot(gy[i], qf[:, i * DH : (i + 1) * DH], 1, 0) for i in range(gy.shape[0])]
    return (jnp.concatenate(states, 0).astype(BF16),)


def mid_body(q, kf, v, g, mixed_local, p):
    qf, q_slope = feature_slope(q)
    normed, gy = normalize(qf, g, mixed_local, p)
    gy = gy[0].T
    mask = causal_mask(q.shape[0])
    m = jnp.where(mask, dot(gy, v, 1, 1), 0.0).astype(BF16)
    a = jnp.where(mask, dot(qf, kf, 1, 1), 0.0).astype(BF16)
    dq = dot(gy, p, 1, 0) + dot(m, kf, 1, 0)
    output = normed[0].astype(BF16).T
    return output, (dq * q_slope).astype(BF16), dot(m, qf, 0, 0).astype(BF16), dot(a, gy, 0, 0).astype(BF16)


def last_body(kf, v, u, dk, dv):
    cuts = [slice(i, i + DH) for i in range(0, u.shape[0], DH)]
    dk = dk.astype(F32) + jnp.concatenate([dot(v[:, h], u[h], 1, 0) for h in cuts], 1)
    dv = dv.astype(F32) + jnp.concatenate([dot(kf[:, h], u[h], 1, 1) for h in cuts], 1)
    return (dk * jnp.minimum(kf.astype(F32), 1.0)).astype(BF16), dv.astype(BF16)


def chunk(ref, at, size, tall):
    piece = pl.ds(pl.multiple_of(at * size, size), size)
    return ref.at[piece, :] if tall else ref.at[:, piece]


def stream_kernel(body, step, together, tall_in, tall_out, held_in, held_out, *refs):
    refs = list(refs)
    take = lambda count: [refs.pop(0) for _ in range(count)]
    ni, no = len(tall_in), len(tall_out)
    ins, outs = take(ni), take(no)
    in_bufs = [r if held else refs.pop(0) for r, held in zip(ins, held_in)]
    out_bufs = [r if held else refs.pop(0) for r, held in zip(outs, held_out)]
    in_sem, out_sem = refs
    moved_in = [i for i in range(ni) if not held_in[i]]
    moved_out = [i for i in range(no) if not held_out[i]]
    size = step * DH
    steps = in_bufs[0].shape[0 if tall_in[0] else 1] // size

    def fetch(i, c):
        return pltpu.make_async_copy(
            chunk(ins[i], c, size, tall_in[i]), chunk(in_bufs[i], c, size, tall_in[i]), in_sem.at[i, c]
        )

    def put(i, c):
        return pltpu.make_async_copy(
            chunk(out_bufs[i], c, size, tall_out[i]), chunk(outs[i], c, size, tall_out[i]), out_sem.at[i, c]
        )

    @pl.loop(0, steps)
    def _(c):
        for i in moved_in:
            fetch(i, c).start()

    @pl.loop(0, steps)
    def _(c):
        for i in moved_in:
            fetch(i, c).wait()
        span = together * DH
        for j in range(step // together):
            at = c * (step // together) + j
            values = [chunk(in_bufs[i], at, span, tall_in[i])[...] for i in range(ni)]
            for i, value in enumerate(body(*values)):
                chunk(out_bufs[i], at, span, tall_out[i])[...] = value
        for i in moved_out:
            put(i, c).start()

    @pl.loop(0, steps)
    def _(c):
        for i in moved_out:
            put(i, c).wait()


def stream(body, name, args, outs, step, flops, held_in=(), held_out=(), together=1):
    width = args[0].shape[1]
    held_in = [i in held_in for i in range(len(args))]
    held_out = [i in held_out for i in range(len(outs))]
    tall_in = [a.shape[0] == width for a in args]
    tall_out = [o.shape[0] == width for o in outs]
    steps = width // DH // step
    nbytes = sum(a.size * a.dtype.itemsize for a in args) + sum(o.size * o.dtype.itemsize for o in outs)
    spec = lambda held: pl.BlockSpec(memory_space=pltpu.VMEM if held else pltpu.HBM)
    place = lambda a, held: pltpu.with_memory_space_constraint(a, pltpu.VMEM if held else pltpu.HBM)
    bufs = [pltpu.VMEM(a.shape, a.dtype) for a, h in zip(args, held_in) if not h]
    bufs += [pltpu.VMEM(o.shape, o.dtype) for o, h in zip(outs, held_out) if not h]
    return pl.pallas_call(
        functools.partial(stream_kernel, body, step, together, tall_in, tall_out, held_in, held_out),
        in_specs=[spec(h) for h in held_in],
        out_specs=[spec(h) for h in held_out],
        out_shape=[(pltpu.VMEM if h else pltpu.HBM)(o.shape, o.dtype) for o, h in zip(outs, held_out)],
        scratch_shapes=bufs
        + [pltpu.SemaphoreType.DMA((len(args), steps)), pltpu.SemaphoreType.DMA((len(outs), steps))],
        name=name,
        compiler_params=pltpu.CompilerParams(vmem_limit_bytes=VMEM_LIMIT),
        cost_estimate=pl.CostEstimate(
            flops=flops * width * args[0].shape[0], bytes_accessed=nbytes, transcendentals=0
        ),
    )(*[place(a, h) for a, h in zip(args, held_in)])


def scan_kernel(n, reverse, x_ref, o_ref, buf, sem):
    r = x_ref.shape[0] // n
    parts = 4 if n % 4 == 0 else 1
    span = n // parts
    total = jnp.zeros((r, DH), F32)
    copies = []
    for part in range(parts):
        for i in range(part * span, (part + 1) * span):
            at = pl.ds((n - 1 - i if reverse else i) * r, r)
            buf[at, :] = total.astype(BF16)
            total = total + x_ref[at, :].astype(F32)
        at = pl.ds((parts - 1 - part if reverse else part) * span * r, span * r)
        copies.append(pltpu.make_async_copy(buf.at[at, :], o_ref.at[at, :], sem.at[part]))
        copies[-1].start()
    for copy in copies:
        copy.wait()


def exclusive_scan(state, n, reverse):
    rows = state.shape[0]
    x = lax.all_to_all(state, AXES, 0, 0, tiled=True)
    y = pl.pallas_call(
        functools.partial(scan_kernel, n, reverse),
        out_shape=pltpu.HBM((rows, DH), BF16),
        in_specs=[pl.BlockSpec(memory_space=pltpu.VMEM)],
        out_specs=pl.BlockSpec(memory_space=pltpu.HBM),
        scratch_shapes=[pltpu.VMEM((rows, DH), BF16), pltpu.SemaphoreType.DMA((4,))],
        name="scan",
        compiler_params=pltpu.CompilerParams(vmem_limit_bytes=VMEM_LIMIT),
    )(pltpu.with_memory_space_constraint(x, pltpu.VMEM))
    return lax.all_to_all(y, AXES, 0, 0, tiled=True)


def local(queries, keys, values, grad_out):
    n = lax.axis_size("seq") * lax.axis_size("head")
    rows, width = queries.shape
    wide = lambda dt: jax.ShapeDtypeStruct((rows, width), dt)
    state = jax.ShapeDtypeStruct((width, DH), BF16)

    turned = jax.ShapeDtypeStruct((width, rows), BF16)
    (own,) = stream(own_body, "own", [keys, values], [state], STEP, 2 * DH, together=STEP)
    prefix = exclusive_scan(own, n, False)
    mixed_local, grad_turned, query_feat, key_feat = stream(
        pre_body, "pre", [queries, keys, values, grad_out], [turned, turned, wide(BF16), wide(BF16)], STEP, 4 * rows, (), (2,)
    )
    (qg,) = stream(fwd_body, "fwd", [query_feat, grad_turned, mixed_local, prefix], [state], STEP, 4 * DH, (0, 3), together=STEP)
    suffix = exclusive_scan(qg, n, True)
    output, grad_q, dk, dv = stream(
        mid_body, "mid", [queries, key_feat, values, grad_turned, mixed_local, prefix], [wide(BF16)] * 4, STEP, 10 * rows, (), (2,)
    )
    grad_k, grad_v = stream(
        last_body, "last", [key_feat, values, suffix, dk, dv], [wide(BF16), wide(BF16)], STEP, 4 * DH, (2, 3), together=STEP
    )
    return (output, grad_q, grad_k, grad_v)


def solution(mesh):
    placed = (P(AXES, None),) * 4
    return jax.shard_map(local, mesh=mesh, in_specs=placed, out_specs=placed, check_vma=False)
```

```python
import functools

import jax
import jax.numpy as jnp
from jax import lax
from jax.experimental import pallas as pl
from jax.experimental.pallas import tpu as pltpu
from jax.sharding import PartitionSpec as P

DH = 128
EPSILON = 1e-06
AXES = ("seq", "head")
F32 = jnp.float32
BF16 = jnp.bfloat16
STEP = 8
VMEM_LIMIT = 24 * 1024 * 1024


def feature(x):
    return jnp.where(x > 0, x + jnp.ones((), BF16), jnp.exp(x.astype(F32)).astype(BF16))


def feature_slope(x):
    xf = x.astype(F32)
    up = xf > 0
    e = jnp.exp(jnp.minimum(xf, 0.0))
    return jnp.where(up, xf + 1.0, e).astype(BF16), jnp.where(up, 1.0, e)


def dot(a, b, ca, cb):
    return lax.dot_general(a, b, (((ca,), (cb,)), ((), ())), preferred_element_type=F32)


def causal_mask(rows):
    t = lax.broadcasted_iota(jnp.int32, (rows, rows), 0)
    s = lax.broadcasted_iota(jnp.int32, (rows, rows), 1)
    return t >= s


def own_body(k, v):
    cuts = [slice(i, i + DH) for i in range(0, k.shape[1], DH)]
    kf = feature(k)
    return (jnp.concatenate([dot(v[:, h], kf[:, h], 0, 0) for h in cuts], 0).astype(BF16),)


def pre_body(q, k, v, g):
    qf = feature(q)
    kf = feature(k)
    a = jnp.where(causal_mask(q.shape[0]), dot(qf, kf, 1, 1), 0.0).astype(BF16)
    return dot(v, a, 0, 1).astype(BF16), g.T, qf, kf


def normalize(qf, g, mixed_local, p):
    cuts = [slice(i, i + DH) for i in range(0, p.shape[0], DH)]
    shape = (len(cuts), DH, qf.shape[0])
    mixed = mixed_local.astype(F32) + jnp.concatenate([dot(p[h], qf[:, h], 1, 1) for h in cuts], 0)
    mixed = mixed.reshape(shape)
    gf = g.astype(F32).reshape(shape)
    inv = lax.rsqrt(jnp.mean(mixed * mixed, 1, keepdims=True) + EPSILON)
    gy = inv * (gf - mixed * (inv * (inv * jnp.mean(gf * mixed, 1, keepdims=True))))
    return mixed * inv, gy.astype(BF16)


def fwd_body(qf, g, mixed_local, p):
    _, gy = normalize(qf, g, mixed_local, p)
    states = [dot(gy[i], qf[:, i * DH : (i + 1) * DH], 1, 0) for i in range(gy.shape[0])]
    return (jnp.concatenate(states, 0).astype(BF16),)


def mid_body(q, kf, v, g, mixed_local, p):
    qf, q_slope = feature_slope(q)
    normed, gy = normalize(qf, g, mixed_local, p)
    gy = gy[0].T
    mask = causal_mask(q.shape[0])
    m = jnp.where(mask, dot(gy, v, 1, 1), 0.0).astype(BF16)
    a = jnp.where(mask, dot(qf, kf, 1, 1), 0.0).astype(BF16)
    dq = dot(gy, p, 1, 0) + dot(m, kf, 1, 0)
    output = normed[0].astype(BF16).T
    return output, (dq * q_slope).astype(BF16), dot(m, qf, 0, 0).astype(BF16), dot(a, gy, 0, 0).astype(BF16)


def last_body(kf, v, u, dk, dv):
    cuts = [slice(i, i + DH) for i in range(0, u.shape[0], DH)]
    dk = dk.astype(F32) + jnp.concatenate([dot(v[:, h], u[h], 1, 0) for h in cuts], 1)
    dv = dv.astype(F32) + jnp.concatenate([dot(kf[:, h], u[h], 1, 1) for h in cuts], 1)
    return (dk * jnp.minimum(kf.astype(F32), 1.0)).astype(BF16), dv.astype(BF16)


def chunk(ref, at, size, tall):
    piece = pl.ds(pl.multiple_of(at * size, size), size)
    return ref.at[piece, :] if tall else ref.at[:, piece]


def stream_kernel(body, step, together, tall_in, tall_out, held_in, held_out, *refs):
    refs = list(refs)
    take = lambda count: [refs.pop(0) for _ in range(count)]
    ni, no = len(tall_in), len(tall_out)
    ins, outs = take(ni), take(no)
    in_bufs = [r if held else refs.pop(0) for r, held in zip(ins, held_in)]
    out_bufs = [r if held else refs.pop(0) for r, held in zip(outs, held_out)]
    in_sem, out_sem = refs
    moved_in = [i for i in range(ni) if not held_in[i]]
    moved_out = [i for i in range(no) if not held_out[i]]
    size = step * DH
    steps = in_bufs[0].shape[0 if tall_in[0] else 1] // size

    def fetch(i, c):
        return pltpu.make_async_copy(
            chunk(ins[i], c, size, tall_in[i]), chunk(in_bufs[i], c, size, tall_in[i]), in_sem.at[i, c]
        )

    span = together * DH
    groups = step // together

    def put(i, at):
        return pltpu.make_async_copy(
            chunk(out_bufs[i], at, span, tall_out[i]), chunk(outs[i], at, span, tall_out[i]), out_sem.at[i, at]
        )

    @pl.loop(0, steps)
    def _(c):
        for i in moved_in:
            fetch(i, c).start()

    @pl.loop(0, steps)
    def _(c):
        for i in moved_in:
            fetch(i, c).wait()
        for j in range(groups):
            at = c * groups + j
            values = [chunk(in_bufs[i], at, span, tall_in[i])[...] for i in range(ni)]
            for i, value in enumerate(body(*values)):
                chunk(out_bufs[i], at, span, tall_out[i])[...] = value
            for i in moved_out:
                put(i, at).start()

    @pl.loop(0, steps * groups)
    def _(at):
        for i in moved_out:
            put(i, at).wait()


def stream(body, name, args, outs, step, flops, held_in=(), held_out=(), together=1):
    width = args[0].shape[1]
    held_in = [i in held_in for i in range(len(args))]
    held_out = [i in held_out for i in range(len(outs))]
    tall_in = [a.shape[0] == width for a in args]
    tall_out = [o.shape[0] == width for o in outs]
    steps = width // DH // step
    nbytes = sum(a.size * a.dtype.itemsize for a in args) + sum(o.size * o.dtype.itemsize for o in outs)
    spec = lambda held: pl.BlockSpec(memory_space=pltpu.VMEM if held else pltpu.HBM)
    place = lambda a, held: pltpu.with_memory_space_constraint(a, pltpu.VMEM if held else pltpu.HBM)
    bufs = [pltpu.VMEM(a.shape, a.dtype) for a, h in zip(args, held_in) if not h]
    bufs += [pltpu.VMEM(o.shape, o.dtype) for o, h in zip(outs, held_out) if not h]
    return pl.pallas_call(
        functools.partial(stream_kernel, body, step, together, tall_in, tall_out, held_in, held_out),
        in_specs=[spec(h) for h in held_in],
        out_specs=[spec(h) for h in held_out],
        out_shape=[(pltpu.VMEM if h else pltpu.HBM)(o.shape, o.dtype) for o, h in zip(outs, held_out)],
        scratch_shapes=bufs
        + [pltpu.SemaphoreType.DMA((len(args), steps)), pltpu.SemaphoreType.DMA((len(outs), width // DH // together))],
        name=name,
        compiler_params=pltpu.CompilerParams(vmem_limit_bytes=VMEM_LIMIT),
        cost_estimate=pl.CostEstimate(
            flops=flops * width * args[0].shape[0], bytes_accessed=nbytes, transcendentals=0
        ),
    )(*[place(a, h) for a, h in zip(args, held_in)])


def scan_kernel(n, reverse, x_ref, o_ref, buf, sem):
    r = x_ref.shape[0] // n
    parts = 8 if n % 8 == 0 else 1
    span = n // parts
    total = jnp.zeros((r, DH), F32)
    copies = []
    for part in range(parts):
        for i in range(part * span, (part + 1) * span):
            at = pl.ds((n - 1 - i if reverse else i) * r, r)
            buf[at, :] = total.astype(BF16)
            total = total + x_ref[at, :].astype(F32)
        at = pl.ds((parts - 1 - part if reverse else part) * span * r, span * r)
        copies.append(pltpu.make_async_copy(buf.at[at, :], o_ref.at[at, :], sem.at[part]))
        copies[-1].start()
    for copy in copies:
        copy.wait()


def exclusive_scan(state, n, reverse):
    rows = state.shape[0]
    x = lax.all_to_all(state, AXES, 0, 0, tiled=True)
    y = pl.pallas_call(
        functools.partial(scan_kernel, n, reverse),
        out_shape=pltpu.HBM((rows, DH), BF16),
        in_specs=[pl.BlockSpec(memory_space=pltpu.VMEM)],
        out_specs=pl.BlockSpec(memory_space=pltpu.HBM),
        scratch_shapes=[pltpu.VMEM((rows, DH), BF16), pltpu.SemaphoreType.DMA((8,))],
        name="scan",
        compiler_params=pltpu.CompilerParams(vmem_limit_bytes=VMEM_LIMIT),
    )(pltpu.with_memory_space_constraint(x, pltpu.VMEM))
    return lax.all_to_all(y, AXES, 0, 0, tiled=True)


def local(queries, keys, values, grad_out):
    n = lax.axis_size("seq") * lax.axis_size("head")
    rows, width = queries.shape
    wide = lambda dt: jax.ShapeDtypeStruct((rows, width), dt)
    state = jax.ShapeDtypeStruct((width, DH), BF16)

    turned = jax.ShapeDtypeStruct((width, rows), BF16)
    (own,) = stream(own_body, "own", [keys, values], [state], STEP, 2 * DH, together=4)
    prefix = exclusive_scan(own, n, False)
    mixed_local, grad_turned, query_feat, key_feat = stream(
        pre_body, "pre", [queries, keys, values, grad_out], [turned, turned, wide(BF16), wide(BF16)], STEP, 4 * rows, (), (2,)
    )
    (qg,) = stream(fwd_body, "fwd", [query_feat, grad_turned, mixed_local, prefix], [state], STEP, 4 * DH, (0, 3), together=STEP)
    suffix = exclusive_scan(qg, n, True)
    output, grad_q, dk, dv = stream(
        mid_body, "mid", [queries, key_feat, values, grad_turned, mixed_local, prefix], [wide(BF16)] * 4, STEP, 10 * rows, (), (2,)
    )
    grad_k, grad_v = stream(
        last_body, "last", [key_feat, values, suffix, dk, dv], [wide(BF16), wide(BF16)], STEP, 4 * DH, (2, 3), together=4
    )
    return (output, grad_q, grad_k, grad_v)


def solution(mesh):
    placed = (P(AXES, None),) * 4
    return jax.shard_map(local, mesh=mesh, in_specs=placed, out_specs=placed, check_vma=False)
```
